512 devices in a mesh: tm: 16 (over x, z_hi, core), space: 32 (over z_lo, y).
Axes of the slice: x: 4, y: 4, z: 16 (z_hi: 2, z_lo: 8; z = z_hi * 8 + z_lo), core: 2. Of those that a mesh axis runs over, the one named last changes fastest.
Arguments:
- snapshots: bfloat16 [32, 128, 4, 2048], P('tm', 'space'), may hold values from -6 to 6
- conv_weight: bfloat16 [32, 4, 3, 3, 3], replicated, may hold values from -0.625 to 0.625
- conv_bias: float32 [32], replicated, may hold values from -3 to 3
- tap_weight: bfloat16 [3, 32, 3, 32], replicated, may hold values from -0.625 to 0.625
- tap_bias: float32 [3, 32], replicated, may hold values from -3 to 3
- mix_weight: bfloat16 [3, 32, 32], replicated, may hold values from -1 to 1
- mix_bias: float32 [3, 32], replicated, may hold values from -3 to 3
Outputs:
- refined: bfloat16 [32, 128, 32, 2048], P('tm', 'space')
The draws below stay inside these ranges and needn't reach their ends.
All inputs are finite; a program needn't handle non-finite values.
Results may differ from the reference program's by a relative error of at most 0.0063.
Values may be sent and summed in bfloat16 or wider, within the bound.
A program may use at most 64 MiB of HBM per device.

```python
import jax
import jax.numpy as jnp
from jax import lax

CIN = 4
CH = 32
LEVELS = 3
XD = 4
NZ = 32
FRAMES = 32
NX = 128
NY = 64


def level_of(stream_key, dims, cuts, least, largest):
    level = 1.0
    for position, parts in cuts:
        heights = jax.random.uniform(jax.random.fold_in(jax.random.fold_in(stream_key, 6), position), (parts,), jnp.float32, least / len(cuts), largest / len(cuts))
        level = level * jnp.repeat(jnp.exp(heights), dims[position] // parts).reshape((-1,) + (1,) * (len(dims) - 1 - position))
    return level


def bell_draw(own_key, extent, width, reach, cuts=(), held_as=jnp.bfloat16):
    entries = width * jax.random.normal(own_key, extent, jnp.float32)
    if cuts:
        entries = entries * level_of(own_key, extent, cuts, -0.22, 0.18)
    return jnp.clip(entries, -reach, reach).astype(held_as)


def setup_inputs(seed: int = 0) -> dict:
    streams_of = jax.random.split(jax.random.key(seed), 8)
    return {
        "snapshots": bell_draw(streams_of[0], (FRAMES, NX, CIN, NY * NZ), 1.0, 6.0, ((0, 16), (1, 32))),
        "conv_weight": bell_draw(streams_of[1], (CH, CIN, 3, 3, 3), (CIN * 27) ** -0.5, 0.625),
        "conv_bias": bell_draw(streams_of[2], (CH,), 0.5, 3.0, (), jnp.float32),
        "tap_weight": bell_draw(streams_of[3], (LEVELS, CH, 3, CH), (3 * CH) ** -0.5, 0.625),
        "tap_bias": bell_draw(streams_of[4], (LEVELS, CH), 0.5, 3.0, (), jnp.float32),
        "mix_weight": bell_draw(streams_of[5], (LEVELS, CH, CH), CH ** -0.5, 1.0),
        "mix_bias": bell_draw(streams_of[6], (LEVELS, CH), 0.5, 3.0, (), jnp.float32),
    }


def spatial_ref(padded, conv_flat, conv_shift):
    frame_count, rows_pad, field_count, lines_pad, depth_count = padded.shape
    row_count = rows_pad - 2
    line_count = lines_pad - 2
    walled = jnp.pad(padded, ((0, 0), (0, 0), (0, 0), (0, 0), (1, 1)))
    pieces = []
    for delta_x in range(3):
        for delta_y in range(3):
            for delta_z in range(3):
                pieces.append(walled[:, delta_x:delta_x + row_count, :, delta_y:delta_y + line_count, delta_z:delta_z + depth_count])
    patches = jnp.stack(pieces, axis=3).reshape(frame_count, row_count, field_count * 27, line_count * depth_count)
    summed = jnp.einsum("ok,fxkc->fxoc", conv_flat.astype(jnp.float32), patches.astype(jnp.float32))
    return jax.nn.gelu(summed + conv_shift[None, None, :, None]).astype(jnp.bfloat16)


def level_ref(current, spacing, tap_flat, tap_shift, mix_flat, mix_shift):
    blank = jnp.zeros((spacing,) + current.shape[1:], current.dtype)
    before = jnp.concatenate([blank, current[:-spacing]], axis=0)
    after = jnp.concatenate([current[spacing:], blank], axis=0)
    stacked = jnp.concatenate([before, current, after], axis=2)
    summed = jnp.einsum("ok,txkc->txoc", tap_flat.astype(jnp.float32), stacked.astype(jnp.float32))
    gated = jax.nn.gelu(summed + tap_shift[None, None, :, None]).astype(jnp.bfloat16)
    gated = lax.optimization_barrier(gated)
    mixed = jnp.einsum("ok,txkc->txoc", mix_flat.astype(jnp.float32), gated.astype(jnp.float32))
    return (current.astype(jnp.float32) + mixed + mix_shift[None, None, :, None]).astype(jnp.bfloat16)


def reference(snapshots, conv_weight, conv_bias, tap_weight, tap_bias, mix_weight, mix_bias):
    frame_total = snapshots.shape[0]
    conv_flat = conv_weight.reshape(CH, CIN * 27)
    tap_flats = tap_weight.reshape(LEVELS, CH, 3 * CH)
    margined = jnp.concatenate([snapshots[:, -1:], snapshots, snapshots[:, :1]], axis=1)

    def block_work(block_index):
        start = (block_index * XD).astype(jnp.int32)
        piece = lax.dynamic_slice_in_dim(margined, start, XD + 2, axis=1)
        shaped = piece.reshape(frame_total, XD + 2, CIN, NY, NZ)
        wrapped = jnp.concatenate([shaped[:, :, :, -1:], shaped, shaped[:, :, :, :1]], axis=3)
        current = spatial_ref(wrapped, conv_flat, conv_bias)
        for level_index in range(LEVELS):
            current = level_ref(current, 2 ** level_index, tap_flats[level_index], tap_bias[level_index], mix_weight[level_index], mix_bias[level_index])
        return current

    blocks = lax.map(block_work, jnp.arange(NX // XD, dtype=jnp.int32))
    return jnp.moveaxis(blocks, 0, 1).reshape(frame_total, NX, CH, NY * NZ)
```

```python
import jax
import jax.numpy as jnp
from jax import lax
from jax.experimental import pallas as pl
from jax.experimental.pallas import tpu as pltpu
from jax.sharding import PartitionSpec as P

F32 = jnp.float32
BF = jnp.bfloat16
MESH = pl.DeviceIdType.MESH
L = 256
NP = 8
K1 = 0.7978845608028654


def prep(conv_weight, tap_weight, mix_weight):
    wt = conv_weight.transpose(0, 3, 4, 2, 1).reshape(32, 9, 3, 4)
    w1 = jnp.stack(
        [
            jnp.pad(wt, ((0, 0), (0, 0), (0, 1), (0, 0))),
            jnp.pad(wt, ((0, 0), (0, 0), (1, 0), (0, 0))),
        ],
        0,
    ).reshape(64, 9, 16)
    i3 = jnp.eye(3, dtype=BF)
    wsp = (i3[:, None, None, :, None] * w1[None, :, :, None, :]).reshape(192, 432)
    band = []
    for s in range(2):
        rows = [
            jnp.pad(tap_weight[s].reshape(32, 96), ((0, 0), (32 * t, 32 * (5 - t))))
            for t in range(6)
        ]
        band.append(jnp.concatenate(rows, 0))
    rows = []
    for t in range(4):
        parts = []
        for tp in range(12):
            k, rest = divmod(tp - t, 4)
            parts.append(
                tap_weight[2][:, k] if rest == 0 and 0 <= k < 3 else jnp.zeros((32, 32), BF)
            )
        rows.append(jnp.concatenate(parts, 1))
    last = jnp.concatenate(rows, 0)
    i8 = jnp.eye(8, dtype=BF)
    mix = (i8[None, :, None, :, None] * mix_weight[:, None, :, None, :]).reshape(3, 256, 256)
    return wsp, jnp.stack(band), last, mix


def gelu(v):
    z = v * (K1 + (K1 * 0.044715) * (v * v))
    h = 0.5 * v
    return h + h * jnp.tanh(z)


def dot(a, b):
    return jnp.dot(a, b, preferred_element_type=F32)


def build_shifts(G, S, k):
    left = lax.rem(2 * k + 15, 16)
    right = lax.rem(2 * k + 2, 16)
    lane = lax.rem(lax.broadcasted_iota(jnp.int32, (16, 512), 1), 32)
    inner_low = lane != 0
    inner_high = lane != 31
    for n in range(18):

        def piece(start, size):
            lanes = pl.ds(pl.multiple_of(start, 128), size)
            return jnp.concatenate([G[n + 1, r, :, lanes].astype(F32) for r in range(4)], 0)

        x = jnp.concatenate(
            [piece(left * 128, 128), piece(k * L, L), piece(right * 128, 128)], 1
        )
        below = jnp.where(inner_low, pltpu.roll(x, 1, 1), 0.0)
        above = jnp.where(inner_high, pltpu.roll(x, 511, 1), 0.0)
        for c, y in enumerate((below, x, above)):
            for b, z in enumerate((pltpu.roll(y, 32, 1), y, pltpu.roll(y, 480, 1))):
                S[3 * b + c, n] = z[:, 128:384].astype(BF)


def spatial(S, H0, wsp, cb):
    for g in range(6):
        acc = dot(wsp[...], S[:, 3 * g : 3 * g + 3].reshape(432, L)).reshape(3, 2, 32, L)
        h = gelu(acc + cb[...]).astype(BF)
        for x in range(2):
            H0[x, 3 * g : 3 * g + 3] = h[:, x]


def blank(q, H, spans):
    for which, (low, high) in spans.items():

        @pl.when(q == which)
        def _():
            H[low:high] = jnp.zeros((high - low,) + H.shape[1:], BF)


def levels(H0, H1, H2, x, band, last, mix, tb, mb, q):
    for o0, no in ((0, 6), (6, 6), (12, 4)):
        xin = H0[x, o0 : o0 + no + 2].reshape((no + 2) * 32, L)
        acc = dot(band[0, : no * 32, : (no + 2) * 32], xin).reshape(no, 32, L)
        g = gelu(acc + tb[0]).astype(BF).reshape(no * 32, L)
        m = dot(mix[0, : no * 32, : no * 32], g).reshape(no, 32, L)
        h = ((H0[x, o0 + 1 : o0 + 1 + no].astype(F32) + m) + mb[0]).astype(BF)
        H1[o0 // 2 : (o0 + no) // 2] = h.reshape(no // 2, 2, 32, L)
    blank(q, H1, {0: (0, 3), 1: (0, 1), 6: (7, 8), 7: (5, 8)})
    for p in range(2):
        xin = H1[:, p]
        acc = dot(band[1], xin.reshape(256, L)).reshape(6, 32, L)
        g = gelu(acc + tb[1]).astype(BF).reshape(192, L)
        m = dot(mix[1, :192, :192], g).reshape(6, 32, L)
        H2[:, p] = ((xin[1:7].astype(F32) + m) + mb[1]).astype(BF)
    blank(q, H2, {0: (0, 2), 7: (4, 6)})
    acc = dot(last[...], H2[...].reshape(384, L)).reshape(4, 32, L)
    g = gelu(acc + tb[2]).astype(BF).reshape(128, L)
    m = dot(mix[2, :128, :128], g).reshape(4, 32, L)
    return ((H2[2:4].reshape(4, 32, L).astype(F32) + m) + mb[2]).astype(BF)


NATIVE, XM, XP, ZB, SB = range(5)


def kernel(snap, wsp, band, last, mix, cb, tb, mb, out, BM, BP, BZ, BS, G, S, H0, H1, H2, O,
           s_z, r_z, s_x, r_x, s_s, r_s, l_g, s_g, r_g, l_o, s_o, r_o):
    tm = lax.axis_index("tm")
    sp = lax.axis_index("space")
    core = lax.rem(tm, 2)
    other = 1 - core
    zh = lax.rem(tm // 2, 2)
    xx = tm // 4
    q = 2 * xx + zh
    n_space = lax.axis_size("space")
    up = lax.rem(sp + 1, n_space)
    down = lax.rem(sp + n_space - 1, n_space)

    def dev(x, z, c, s):
        return (lax.rem(x + 4, 4) * 4 + z * 2 + c, s)

    z_dev = dev(xx, 1 - zh, core, sp)
    xm_dev = dev(xx + 3, zh, core, sp)
    xp_dev = dev(xx + 1, zh, core, sp)
    relay_dev = dev(xx + 1 + 2 * zh, zh, core, sp)
    core_dev = dev(xx, zh, other, sp)
    up_dev = dev(xx, zh, 0, up)
    down_dev = dev(xx, zh, 1, down)
    side = jnp.where(core == 0, down, up)
    side_dev = dev(xx, zh, core, side)

    barrier = pltpu.get_barrier_semaphore()
    for d in (z_dev, xm_dev, xp_dev, core_dev, up_dev, down_dev, side_dev):
        pl.semaphore_signal(barrier, inc=1, device_id=d, device_id_type=MESH)
    pl.semaphore_wait(barrier, 7)

    def remote(src, dst, send, recv, d):
        return pltpu.make_async_remote_copy(
            src_ref=src, dst_ref=dst, send_sem=send, recv_sem=recv, device_id=d,
            device_id_type=MESH,
        )

    def lanes(k):
        return pl.ds(pl.multiple_of(k * L, L), L)

    def z_copy(k):
        return remote(snap.at[:, :, :, lanes(k)], BZ.at[:, :, :, lanes(k)], s_z.at[k], r_z.at[k], z_dev)

    def s_copy(k):
        return remote(BZ.at[:, :, :, lanes(k)], BS.at[:, :, :, lanes(k)], s_s.at[k], r_s.at[k], relay_dev)

    def xm_copy():
        return remote(snap, BP, s_x.at[0], r_x.at[0], xm_dev)

    def xp_copy():
        return remote(snap, BM, s_x.at[1], r_x.at[1], xp_dev)

    slot_of = {NATIVE: 2, XM: 0, XP: 4, ZB: 3 - 2 * zh, SB: 1 + 2 * zh}
    buffer_of = {NATIVE: snap, XM: BM, XP: BP, ZB: BZ, SB: BS}

    def copies(kind, k, whole):
        b = buffer_of[kind]
        first = 4 * slot_of[kind] + 2 * core
        ln = pl.ds(0, 2048) if whole else lanes(k)
        fr = pl.ds(first, 2)
        i = 8 * kind + k
        local = pltpu.make_async_copy(
            b.at[:, pl.ds(core, 3), :, ln], G.at[fr, pl.ds(1 - core, 3), :, ln], l_g.at[i]
        )
        to_core = remote(
            b.at[:, pl.ds(other, 3), :, ln], G.at[fr, pl.ds(core, 3), :, ln],
            s_g.at[i, 0], r_g.at[i, 0], core_dev,
        )
        to_up = remote(
            b.at[:, 3, :, ln], G.at[fr, 0, :, ln], s_g.at[i, 1], r_g.at[i, 1 + core], up_dev
        )
        to_down = remote(
            b.at[:, 0, :, ln], G.at[fr, 3, :, ln], s_g.at[i, 2], r_g.at[i, 1 + core], down_dev
        )
        return local, to_core, to_up, to_down

    def spread(kind, k=0, whole=False):
        local, to_core, to_up, to_down = copies(kind, k, whole)
        to_core.start()
        to_up.start()
        to_down.start()
        local.start()

    def settle(kind, k=0, whole=False):
        i = 8 * kind + k
        ln = pl.ds(0, 2048) if whole else lanes(k)
        first = 4 * slot_of[kind]
        copies(kind, k, whole)[0].wait()
        theirs = G.at[pl.ds(first + 2 * other, 2), pl.ds(1 - core, 3), :, ln]
        remote(theirs, theirs, s_g.at[i, 0], r_g.at[i, 0], core_dev).wait_recv()
        for c in range(2):
            row = G.at[pl.ds(first + 2 * c, 2), 3 * core, :, ln]
            remote(row, row, s_g.at[i, 1], r_g.at[i, 1 + c], side_dev).wait_recv()

    def sent(kind, k=0, whole=False):
        for c in copies(kind, k, whole)[1:]:
            c.wait_send()

    def take_z(k):
        z_copy(k).wait_recv()
        s_copy(k).start()
        spread(ZB, k)

    def take_s(k):
        s_copy(k).wait_recv()
        spread(SB, k)

    @pl.loop(0, NP)
    def _(k):
        z_copy(k).start()

    xm_copy().start()
    xp_copy().start()
    spread(NATIVE, 0, True)
    xp_copy().wait_recv()
    spread(XM, 0, True)
    xm_copy().wait_recv()
    spread(XP, 0, True)
    for kind in (NATIVE, XM, XP):
        settle(kind, 0, True)

    @pl.loop(0, 3)
    def _(k):
        take_z(k)

    @pl.loop(0, 2)
    def _(k):
        take_s(k)

    take_z(3)
    take_s(2)

    @pl.loop(0, 2)
    def _(k):
        settle(ZB, k)
        settle(SB, k)

    def out_copies(k):
        mine = pltpu.make_async_copy(
            O.at[k, pl.ds(2 * core, 2)], out.at[:, pl.ds(2 * core, 2), :, lanes(k)], l_o.at[k]
        )
        theirs = remote(
            O.at[k, pl.ds(2 * other, 2)], out.at[:, pl.ds(2 * core, 2), :, lanes(k)],
            s_o.at[k], r_o.at[k], core_dev,
        )
        return mine, theirs

    @pl.loop(0, NP)
    def _(i):
        @pl.when(i + 4 < NP)
        def _():
            take_z(i + 4)

        @pl.when(i + 3 < NP)
        def _():
            take_s(i + 3)

        @pl.when(i + 2 < NP)
        def _():
            settle(ZB, i + 2)
            settle(SB, i + 2)

        k = lax.rem(i + 1, NP)
        build_shifts(G, S, k)
        spatial(S, H0, wsp, cb)
        for x in range(2):
            blank(q, H0.at[x], {0: (0, 7), 1: (0, 3), 6: (15, 18), 7: (11, 18)})
            O[k, :, x] = levels(H0, H1, H2, x, band, last, mix, tb, mb, q)
        mine, theirs = out_copies(k)
        mine.start()
        theirs.start()

    xm_copy().wait_send()
    xp_copy().wait_send()
    for kind in (NATIVE, XM, XP):
        sent(kind, 0, True)

    @pl.loop(0, NP)
    def _(k):
        z_copy(k).wait_send()
        s_copy(k).wait_send()
        sent(ZB, k)
        sent(SB, k)
        mine, theirs = out_copies(k)
        mine.wait()
        theirs.wait_send()
        into = out.at[:, pl.ds(2 * other, 2), :, lanes(k)]
        remote(into, into, s_o.at[k], r_o.at[k], core_dev).wait_recv()


def shards(snapshots, conv_weight, conv_bias, tap_weight, tap_bias, mix_weight, mix_bias):
    wsp, band, last, mix = prep(conv_weight, tap_weight, mix_weight)
    vm = pl.BlockSpec(memory_space=pltpu.VMEM)
    anywhere = pl.BlockSpec(memory_space=pl.ANY)
    dma = pltpu.SemaphoreType.DMA
    return pl.pallas_call(
        kernel,
        out_shape=jax.ShapeDtypeStruct((2, 4, 32, 2048), BF),
        in_specs=[anywhere] + [vm] * 7,
        out_specs=anywhere,
        scratch_shapes=[pltpu.VMEM((2, 4, 4, 2048), BF)] * 4
        + [
            pltpu.VMEM((20, 4, 4, 2048), BF),
            pltpu.VMEM((9, 18, 16, L), BF),
            pltpu.VMEM((2, 18, 32, L), BF),
            pltpu.VMEM((8, 2, 32, L), BF),
            pltpu.VMEM((6, 2, 32, L), BF),
            pltpu.VMEM((NP, 4, 2, 32, L), BF),
            dma((NP,)), dma((NP,)), dma((2,)), dma((2,)), dma((NP,)), dma((NP,)),
            dma((40,)), dma((40, 3)), dma((40, 3)),
            dma((NP,)), dma((NP,)), dma((NP,)),
        ],
        compiler_params=pltpu.CompilerParams(
            collective_id=0, has_side_effects=True, vmem_limit_bytes=56 << 20
        ),
        name="encoder",
    )(snapshots, wsp, band, last, mix, conv_bias[:, None], tap_bias[:, :, None], mix_bias[:, :, None])


def solution(mesh):
    in_specs = (P("tm", "space", None, None), P(), P(), P(), P(), P(), P())
    out_specs = P("tm", "space", None, None)
    return jax.shard_map(shards, mesh=mesh, in_specs=in_specs, out_specs=out_specs, check_vma=False)
```

```python
import jax
import jax.numpy as jnp
from jax import lax
from jax.experimental import pallas as pl
from jax.experimental.pallas import tpu as pltpu
from jax.sharding import PartitionSpec as P

F32 = jnp.float32
BF = jnp.bfloat16
MESH = pl.DeviceIdType.MESH
L = 256
NP = 8
K1 = 0.7978845608028654


def iota(shape, dim):
    return lax.broadcasted_iota(jnp.int32, shape, dim)


def dot(a, b):
    return jnp.dot(a, b, preferred_element_type=F32)


def chosen(condition):
    return jnp.where(condition, 1.0, 0.0).astype(BF)


def prepare(flat, mixw, cb, tb, mb, wsp, band, last, mix, bias):
    j = iota((128, 144), 0)
    col = iota((128, 144), 1)
    field_row = (j * 57) >> 9
    field = (field_row * 11) >> 5
    shift = field_row - 3 * field
    match = ((j - 9 * field_row) == (col >> 4)) & (field == (col & 3)) & (j < 108)
    rows = []
    for x in range(2):
        rows.append(dot(flat[0], chosen(match & (shift == ((col >> 2) & 3) - x))))
    wsp[...] = jnp.concatenate(rows, 0).astype(BF)

    def banded(weights, step, outs, ins):
        j = iota((128, 32 * ins), 0)
        col = iota((128, 32 * ins), 1)
        gap = (iota((32 * outs, 32 * ins), 1) >> 5) - (iota((32 * outs, 32 * ins), 0) >> 5)
        total = jnp.zeros((32 * outs, 32 * ins), F32)
        for k in range(3):
            picked = dot(weights, chosen(j == 32 * k + (col & 31)))
            total = jnp.where(gap == k * step, jnp.concatenate([picked] * outs, 0), total)
        return total.astype(BF)

    for s in range(2):
        band[s] = banded(flat[1 + s], 1, 6, 8)
    last[...] = banded(flat[3], 4, 4, 12)
    spread = chosen(iota((32, 256), 0) == (iota((32, 256), 1) & 31))
    same = (iota((256, 256), 0) >> 5) == (iota((256, 256), 1) >> 5)
    for s in range(3):
        tiled = jnp.concatenate([dot(mixw[s], spread)] * 8, 0)
        mix[s] = jnp.where(same, tiled, 0.0).astype(BF)
    unit = iota((32, 32), 0) == iota((32, 32), 1)
    rows = [cb[...]] + [b[n : n + 1, :] for b in (tb, mb) for n in range(3)]
    for n in range(7):
        row = jnp.where(unit, jnp.broadcast_to(rows[n], (32, 32)), 0.0)
        bias[n] = jnp.broadcast_to(jnp.sum(row, 1, keepdims=True), (32, L))


def gelu(v):
    z = v * (K1 + (K1 * 0.044715) * (v * v))
    h = 0.5 * v
    return h + h * jnp.tanh(z)


def features(G, H0, k, frames, wsp, bias, q):
    left = lax.rem(2 * k + 15, 16)
    right = lax.rem(2 * k + 2, 16)
    lane = lax.rem(iota((16, 512), 1), 32)
    inner_low = lane != 0
    inner_high = lane != 31
    for n in frames:

        def piece(start, size):
            lanes = pl.ds(pl.multiple_of(start, 128), size)
            return jnp.concatenate([G[n + 1, r, :, lanes].astype(F32) for r in range(4)], 0)

        x = jnp.concatenate(
            [piece(left * 128, 128), piece(k * L, L), piece(right * 128, 128)], 1
        )
        below = jnp.where(inner_low, pltpu.roll(x, 1, 1), 0.0)
        above = jnp.where(inner_high, pltpu.roll(x, 511, 1), 0.0)
        moved = [(pltpu.roll(y, 32, 1), y, pltpu.roll(y, 480, 1)) for y in (below, x, above)]
        taps = [moved[c][b][:, 128:384].astype(BF) for b in range(3) for c in range(3)]
        acc = dot(wsp[...], jnp.concatenate(taps, 0)).reshape(2, 32, L)
        h = gelu(acc + bias[0]).astype(BF)
        for x in range(2):
            H0[k, x, n] = h[x]
    for which, (low, high) in SPANS.items():

        @pl.when(q == which)
        def _():
            for x in range(2):
                H0[k, x, low:high] = jnp.zeros((high - low, 32, L), BF)


def blank(q, H, spans):
    for which, (low, high) in spans.items():

        @pl.when(q == which)
        def _():
            H[low:high] = jnp.zeros((high - low,) + H.shape[1:], BF)


def levels(H0, H1, H2, band, last, mix, bias, q):
    for o0, no in ((0, 6), (6, 6), (12, 4)):
        xin = H0[o0 : o0 + no + 2].reshape((no + 2) * 32, L)
        acc = dot(band[0, : no * 32, : (no + 2) * 32], xin).reshape(no, 32, L)
        g = gelu(acc + bias[1]).astype(BF).reshape(no * 32, L)
        m = dot(mix[0, : no * 32, : no * 32], g).reshape(no, 32, L)
        h = ((H0[o0 + 1 : o0 + 1 + no].astype(F32) + m) + bias[4]).astype(BF)
        H1[o0 // 2 : (o0 + no) // 2] = h.reshape(no // 2, 2, 32, L)
    blank(q, H1, {0: (0, 3), 1: (0, 1), 6: (7, 8), 7: (5, 8)})
    for p in range(2):
        xin = H1[:, p]
        acc = dot(band[1], xin.reshape(256, L)).reshape(6, 32, L)
        g = gelu(acc + bias[2]).astype(BF).reshape(192, L)
        m = dot(mix[1, :192, :192], g).reshape(6, 32, L)
        H2[:, p] = ((xin[1:7].astype(F32) + m) + bias[5]).astype(BF)
    blank(q, H2, {0: (0, 2), 7: (4, 6)})
    acc = dot(last[...], H2[...].reshape(384, L)).reshape(4, 32, L)
    g = gelu(acc + bias[3]).astype(BF).reshape(128, L)
    m = dot(mix[2, :128, :128], g).reshape(4, 32, L)
    return ((H2[2:4].reshape(4, 32, L).astype(F32) + m) + bias[6]).astype(BF)


NATIVE, XM, XP, ZB, SB = range(5)
OWN = (0, 1, 2, 7, 8, 9, 10, 15, 16, 17)
FAR = (3, 4, 5, 6, 11, 12, 13, 14)
SPANS = {0: (0, 7), 1: (0, 3), 6: (15, 18), 7: (11, 18)}


def kernel(snap, flat, mixw, cb, tb, mb, out, BM, BP, BZ, BS, G, O, wsp, band, last, mix, bias, H0, H1, H2,
           s_z, r_z, s_x, r_x, s_s, r_s, l_g, s_g, r_g, l_o, s_o, r_o):
    tm = lax.axis_index("tm")
    sp = lax.axis_index("space")
    core = lax.rem(tm, 2)
    other = 1 - core
    zh = lax.rem(tm // 2, 2)
    xx = tm // 4
    q = 2 * xx + zh
    top = lax.axis_size("space") - 1
    up = jnp.where(sp == top, 0, sp + 1)
    down = jnp.where(sp == 0, top, sp - 1)

    def dev(x, z, c, s):
        return (lax.rem(x, 4) * 4 + z * 2 + c, s)

    z_dev = dev(xx, 1 - zh, core, sp)
    xm_dev = dev(xx + 3, zh, core, sp)
    xp_dev = dev(xx + 1, zh, core, sp)
    relay_dev = dev(xx + 1 + 2 * zh, zh, core, sp)
    core_dev = dev(xx, zh, other, sp)
    up_dev = dev(xx, zh, 0, up)
    down_dev = dev(xx, zh, 1, down)
    side_dev = dev(xx, zh, core, jnp.where(core == 0, down, up))
    far_up = dev(xx, 1 - zh, 0, up)
    far_down = dev(xx, 1 - zh, 1, down)

    barrier = pltpu.get_barrier_semaphore()

    def greet(d):
        pl.semaphore_signal(barrier, inc=1, device_id=d, device_id_type=MESH)

    for d in (z_dev, xm_dev, xp_dev, core_dev, up_dev, down_dev, side_dev):
        greet(d)

    @pl.when(sp == top)
    def _():
        greet(far_up)

    @pl.when((sp == top) & (core == 1))
    def _():
        greet(dev(xx, 1 - zh, 1, up))

    @pl.when(sp == 0)
    def _():
        greet(far_down)

    @pl.when((sp == 0) & (core == 0))
    def _():
        greet(dev(xx, 1 - zh, 0, down))

    more = jnp.where(sp == top, 1 + core, 0) + jnp.where(sp == 0, 2 - core, 0)
    pl.semaphore_wait(barrier, 7 + more)

    def remote(src, dst, send, recv, d):
        return pltpu.make_async_remote_copy(
            src_ref=src, dst_ref=dst, send_sem=send, recv_sem=recv, device_id=d,
            device_id_type=MESH,
        )

    def lanes(k):
        return pl.ds(pl.multiple_of(k * L, L), L)

    def z_copy(k):
        ln = lanes(k)
        return remote(snap.at[:, :, :, ln], BZ.at[:, :, :, ln], s_z.at[k], r_z.at[k], z_dev)

    def s_copy(k):
        ln = lanes(k)
        return remote(BZ.at[:, :, :, ln], BS.at[:, :, :, ln], s_s.at[k], r_s.at[k], relay_dev)

    def xm_copy():
        return remote(snap, BP, s_x.at[0], r_x.at[0], xm_dev)

    def xp_copy():
        return remote(snap, BM, s_x.at[1], r_x.at[1], xp_dev)

    slot_of = {NATIVE: 2, XM: 0, XP: 4, ZB: 3 - 2 * zh, SB: 1 + 2 * zh}
    buffer_of = {NATIVE: snap, XM: BM, XP: BP, ZB: BZ, SB: BS}

    def span(kind, k):
        return pl.ds(0, 2048) if kind in (NATIVE, XM, XP) else lanes(k)

    def frames_of(kind, c):
        return pl.ds(4 * slot_of[kind] + 2 * c, 2)

    def local_copy(kind, k):
        ln = span(kind, k)
        return pltpu.make_async_copy(
            buffer_of[kind].at[:, pl.ds(core, 3), :, ln],
            G.at[frames_of(kind, core), pl.ds(1 - core, 3), :, ln], l_g.at[8 * kind + k],
        )

    def core_copy(kind, k):
        ln, i = span(kind, k), 8 * kind + k
        return remote(
            buffer_of[kind].at[:, pl.ds(other, 3), :, ln],
            G.at[frames_of(kind, core), pl.ds(core, 3), :, ln],
            s_g.at[i, 0], r_g.at[i, 0], core_dev,
        )

    def up_copy(kind, k):
        ln, i = span(kind, k), 8 * kind + k
        return remote(
            buffer_of[kind].at[:, 3, :, ln], G.at[frames_of(kind, core), 0, :, ln],
            s_g.at[i, 1], r_g.at[i, 1 + core], up_dev,
        )

    def down_copy(kind, k):
        ln, i = span(kind, k), 8 * kind + k
        return remote(
            buffer_of[kind].at[:, 0, :, ln], G.at[frames_of(kind, core), 3, :, ln],
            s_g.at[i, 2], r_g.at[i, 1 + core], down_dev,
        )

    def far_copies(source, kind):
        slot = 1 + 2 * zh if kind == ZB else 3 - 2 * zh
        fr = pl.ds(4 * slot + 2 * core, 2)

        @pl.when(sp == top)
        def _():
            @pl.loop(0, NP)
            def _(k):
                i = 8 * kind + k
                remote(
                    source.at[:, 3, :, lanes(k)], G.at[fr, 0, :, lanes(k)],
                    s_g.at[i, 1], r_g.at[i, 1 + core], far_up,
                ).start()

        @pl.when(sp == 0)
        def _():
            @pl.loop(0, NP)
            def _(k):
                i = 8 * kind + k
                remote(
                    source.at[:, 0, :, lanes(k)], G.at[fr, 3, :, lanes(k)],
                    s_g.at[i, 2], r_g.at[i, 1 + core], far_down,
                ).start()

    def spread(kind, k=0):
        core_copy(kind, k).start()
        if kind in (NATIVE, XM, XP):
            up_copy(kind, k).start()
            down_copy(kind, k).start()
        else:

            @pl.when(sp != top)
            def _():
                up_copy(kind, k).start()

            @pl.when(sp != 0)
            def _():
                down_copy(kind, k).start()

        local_copy(kind, k).start()

    def settle(kind, k=0):
        ln, i = span(kind, k), 8 * kind + k
        local_copy(kind, k).wait()
        theirs = G.at[frames_of(kind, other), pl.ds(1 - core, 3), :, ln]
        remote(theirs, theirs, s_g.at[i, 0], r_g.at[i, 0], core_dev).wait_recv()
        for c in range(2):
            row = G.at[frames_of(kind, c), 3 * core, :, ln]
            remote(row, row, s_g.at[i, 1], r_g.at[i, 1 + c], side_dev).wait_recv()

    def sent(kind, k=0):
        core_copy(kind, k).wait_send()
        up_copy(kind, k).wait_send()
        down_copy(kind, k).wait_send()

    def take_z(k):
        z_copy(k).wait_recv()
        s_copy(k).start()
        spread(ZB, k)

    def take_s(k):
        s_copy(k).wait_recv()
        spread(SB, k)

    def settle_far(k):
        settle(ZB, k)
        settle(SB, k)

    def out_copies(k):
        mine = pltpu.make_async_copy(
            O.at[k, pl.ds(2 * core, 2)], out.at[:, pl.ds(2 * core, 2), :, lanes(k)], l_o.at[k]
        )
        theirs = remote(
            O.at[k, pl.ds(2 * other, 2)], out.at[:, pl.ds(2 * core, 2), :, lanes(k)],
            s_o.at[k], r_o.at[k], core_dev,
        )
        return mine, theirs

    @pl.loop(0, NP)
    def _(k):
        z_copy(k).start()

    xm_copy().start()
    xp_copy().start()
    spread(NATIVE)
    far_copies(snap, ZB)
    prepare(flat, mixw, cb, tb, mb, wsp, band, last, mix, bias)
    xp_copy().wait_recv()
    spread(XM)
    xm_copy().wait_recv()
    spread(XP)

    @pl.when(zh == 0)
    def _():
        far_copies(BP, SB)

    @pl.when(zh == 1)
    def _():
        far_copies(BM, SB)

    for kind in (NATIVE, XM, XP):
        settle(kind)

    @pl.loop(0, NP)
    def _(i):
        features(G, H0, i, OWN, wsp, bias, q)

        @pl.when(i >= 1)
        def _():
            take_z(i - 1)

        @pl.when(i >= 3)
        def _():
            take_s(i - 3)

    take_z(NP - 1)
    take_s(NP - 3)
    settle_far(0)
    settle_far(1)

    @pl.loop(0, NP)
    def _(i):
        @pl.when(i + 6 < NP)
        def _():
            take_s(i + 6)

        @pl.when(i + 2 < NP)
        def _():
            settle_far(i + 2)

        k = lax.rem(i + 1, NP)
        features(G, H0, k, FAR, wsp, bias, q)
        for x in range(2):
            O[k, :, x] = levels(H0.at[k, x], H1, H2, band, last, mix, bias, q)
        mine, theirs = out_copies(k)
        mine.start()
        theirs.start()

    xm_copy().wait_send()
    xp_copy().wait_send()
    for kind in (NATIVE, XM, XP):
        sent(kind)

    @pl.loop(0, NP)
    def _(k):
        z_copy(k).wait_send()
        s_copy(k).wait_send()
        sent(ZB, k)
        sent(SB, k)
        mine, theirs = out_copies(k)
        mine.wait()
        theirs.wait_send()
        into = out.at[:, pl.ds(2 * other, 2), :, lanes(k)]
        remote(into, into, s_o.at[k], r_o.at[k], core_dev).wait_recv()


def shards(snapshots, conv_weight, conv_bias, tap_weight, tap_bias, mix_weight, mix_bias):
    flat = jnp.concatenate(
        [
            jnp.pad(conv_weight.reshape(1, 32, 108), ((0, 0), (0, 0), (0, 20))),
            jnp.pad(tap_weight.reshape(3, 32, 96), ((0, 0), (0, 0), (0, 32))),
        ],
        0,
    )
    vm = pl.BlockSpec(memory_space=pltpu.VMEM)
    anywhere = pl.BlockSpec(memory_space=pl.ANY)
    dma = pltpu.SemaphoreType.DMA
    return pl.pallas_call(
        kernel,
        out_shape=jax.ShapeDtypeStruct((2, 4, 32, 2048), BF),
        in_specs=[anywhere] + [vm] * 5,
        out_specs=anywhere,
        scratch_shapes=[pltpu.VMEM((2, 4, 4, 2048), BF)] * 4
        + [
            pltpu.VMEM((20, 4, 4, 2048), BF),
            pltpu.VMEM((NP, 4, 2, 32, L), BF),
            pltpu.VMEM((64, 144), BF),
            pltpu.VMEM((2, 192, 256), BF),
            pltpu.VMEM((128, 384), BF),
            pltpu.VMEM((3, 256, 256), BF),
            pltpu.VMEM((7, 32, L), F32),
            pltpu.VMEM((NP, 2, 18, 32, L), BF),
            pltpu.VMEM((8, 2, 32, L), BF),
            pltpu.VMEM((6, 2, 32, L), BF),
            dma((NP,)), dma((NP,)), dma((2,)), dma((2,)), dma((NP,)), dma((NP,)),
            dma((40,)), dma((40, 3)), dma((40, 3)),
            dma((NP,)), dma((NP,)), dma((NP,)),
        ],
        compiler_params=pltpu.CompilerParams(
            collective_id=0, has_side_effects=True, vmem_limit_bytes=56 << 20
        ),
        name="encoder",
    )(snapshots, flat, mix_weight, conv_bias[None], tap_bias, mix_bias)


def solution(mesh):
    in_specs = (P("tm", "space", None, None), P(), P(), P(), P(), P(), P())
    out_specs = P("tm", "space", None, None)
    return jax.shard_map(shards, mesh=mesh, in_specs=in_specs, out_specs=out_specs, check_vma=False)
```

```python
import jax
import jax.numpy as jnp
from jax import lax
from jax.experimental import pallas as pl
from jax.experimental.pallas import tpu as pltpu
from jax.sharding import PartitionSpec as P

F32 = jnp.float32
BF = jnp.bfloat16
MESH = pl.DeviceIdType.MESH
L = 256
NP = 8
K1 = 0.7978845608028654


def iota(shape, dim):
    return lax.broadcasted_iota(jnp.int32, shape, dim)


def dot(a, b):
    return jnp.dot(a, b, preferred_element_type=F32)


def chosen(condition):
    return jnp.where(condition, 1.0, 0.0).astype(BF)


def prepare(q, flat, mixw, cb, tb, mb, wsp, band, last, mix, bias):
    j = iota((128, 144), 0)
    col = iota((128, 144), 1)
    field_row = (j * 57) >> 9
    field = (field_row * 11) >> 5
    shift = field_row - 3 * field
    match = ((j - 9 * field_row) == (col >> 4)) & (field == (col & 3)) & (j < 108)
    rows = []
    for x in range(2):
        rows.append(dot(flat[0], chosen(match & (shift == ((col >> 2) & 3) - x))))
    wsp[...] = (0.5 * jnp.concatenate(rows, 0)).astype(BF)

    def banded(weights, step, outs, ins, first, stride):
        j = iota((128, 32 * ins), 0)
        col = iota((128, 32 * ins), 1)
        gap = (iota((32 * outs, 32 * ins), 1) >> 5) - (iota((32 * outs, 32 * ins), 0) >> 5)
        total = jnp.zeros((32 * outs, 32 * ins), F32)
        for k in range(3):
            picked = dot(weights, chosen(j == 32 * k + (col & 31)))
            total = jnp.where(gap == k * step, jnp.concatenate([picked] * outs, 0), total)
        frame = first + stride * (iota((32 * outs, 32 * ins), 1) >> 5)
        return (0.5 * jnp.where((frame >= 0) & (frame < 32), total, 0.0)).astype(BF)

    for g in range(3):
        band[g] = banded(flat[1], 1, 6, 8, 4 * q - 7 + 6 * g, 1)
    for p in range(2):
        band[3 + p] = banded(flat[2], 1, 6, 8, 4 * q - 6 + p, 2)
    last[...] = banded(flat[3], 4, 4, 12, 4 * q - 4, 1)
    spread = chosen(iota((32, 256), 0) == (iota((32, 256), 1) & 31))
    same = (iota((256, 256), 0) >> 5) == (iota((256, 256), 1) >> 5)
    for s in range(3):
        tiled = jnp.concatenate([dot(mixw[s], spread)] * 8, 0)
        mix[s] = jnp.where(same, tiled, 0.0).astype(BF)
    unit = iota((32, 32), 0) == iota((32, 32), 1)
    rows = [0.5 * cb[...]] + [0.5 * tb[n : n + 1, :] for n in range(3)]
    rows += [mb[n : n + 1, :] for n in range(3)]
    for n in range(7):
        row = jnp.where(unit, jnp.broadcast_to(rows[n], (32, 32)), 0.0)
        bias[n] = jnp.broadcast_to(jnp.sum(row, 1, keepdims=True), (32, L))


def gelu(h):
    return h + h * jnp.tanh(h * (2 * K1 + (8 * K1 * 0.044715) * (h * h)))


def features(G, H0, k, frames, wsp, bias):
    left = lax.rem(2 * k + 15, 16)
    right = lax.rem(2 * k + 2, 16)
    lane = lax.rem(iota((16, 512), 1), 32)
    inner_low = lane != 0
    inner_high = lane != 31
    for n in frames:

        def piece(start, size):
            lanes = pl.ds(pl.multiple_of(start, 128), size)
            return jnp.concatenate([G[n + 1, r, :, lanes].astype(F32) for r in range(4)], 0)

        x = jnp.concatenate(
            [piece(left * 128, 128), piece(k * L, L), piece(right * 128, 128)], 1
        )
        below = jnp.where(inner_low, pltpu.roll(x, 1, 1), 0.0)
        above = jnp.where(inner_high, pltpu.roll(x, 511, 1), 0.0)
        moved = [(pltpu.roll(y, 32, 1), y, pltpu.roll(y, 480, 1)) for y in (below, x, above)]
        taps = [moved[c][b][:, 128:384].astype(BF) for b in range(3) for c in range(3)]
        acc = dot(wsp[...], jnp.concatenate(taps, 0)).reshape(2, 32, L)
        h = gelu(acc + bias[0]).astype(BF)
        for x in range(2):
            H0[k, x, n] = h[x]


def levels(H0, H1, H2, O, band, last, mix, bias):
    for o0, no in ((0, 6), (6, 6), (12, 4)):
        for x in range(2):
            xin = H0[x, o0 : o0 + no + 2].reshape((no + 2) * 32, L)
            acc = dot(band[o0 // 6, : no * 32, : (no + 2) * 32], xin).reshape(no, 32, L)
            g = gelu(acc + bias[1]).astype(BF).reshape(no * 32, L)
            m = dot(mix[0, : no * 32, : no * 32], g).reshape(no, 32, L)
            h = ((H0[x, o0 + 1 : o0 + 1 + no].astype(F32) + m) + bias[4]).astype(BF)
            H1[x, o0 // 2 : (o0 + no) // 2] = h.reshape(no // 2, 2, 32, L)
    for p in range(2):
        for x in range(2):
            xin = H1[x, :, p]
            acc = dot(band[3 + p], xin.reshape(256, L)).reshape(6, 32, L)
            g = gelu(acc + bias[2]).astype(BF).reshape(192, L)
            m = dot(mix[1, :192, :192], g).reshape(6, 32, L)
            H2[x, :, p] = ((xin[1:7].astype(F32) + m) + bias[5]).astype(BF)
    for x in range(2):
        acc = dot(last[...], H2[x].reshape(384, L)).reshape(4, 32, L)
        g = gelu(acc + bias[3]).astype(BF).reshape(128, L)
        m = dot(mix[2, :128, :128], g).reshape(4, 32, L)
        O[:, x] = ((H2[x, 2:4].reshape(4, 32, L).astype(F32) + m) + bias[6]).astype(BF)


NATIVE, XM, XP, ZB, SB = range(5)
OWN = (0, 1, 2, 7, 8, 9, 10, 15, 16, 17)
FAR = (3, 4, 5, 6, 11, 12, 13, 14)


def kernel(snap, flat, mixw, cb, tb, mb, out, BM, BP, BZ, BS, G, O, wsp, band, last, mix, bias, H0, H1, H2,
           s_z, r_z, s_x, r_x, s_s, r_s, l_g, s_g, r_g, l_o, s_o, r_o):
    tm = lax.axis_index("tm")
    sp = lax.axis_index("space")
    core = lax.rem(tm, 2)
    other = 1 - core
    zh = lax.rem(tm // 2, 2)
    xx = tm // 4
    q = 2 * xx + zh
    top = lax.axis_size("space") - 1
    up = jnp.where(sp == top, 0, sp + 1)
    down = jnp.where(sp == 0, top, sp - 1)

    def dev(x, z, c, s):
        return (lax.rem(x, 4) * 4 + z * 2 + c, s)

    z_dev = dev(xx, 1 - zh, core, sp)
    xm_dev = dev(xx + 3, zh, core, sp)
    xp_dev = dev(xx + 1, zh, core, sp)
    relay_dev = dev(xx + 1 + 2 * zh, zh, core, sp)
    core_dev = dev(xx, zh, other, sp)
    up_dev = dev(xx, zh, 0, up)
    down_dev = dev(xx, zh, 1, down)
    side_dev = dev(xx, zh, core, jnp.where(core == 0, down, up))
    far_up = dev(xx, 1 - zh, 0, up)
    far_down = dev(xx, 1 - zh, 1, down)

    barrier = pltpu.get_barrier_semaphore()

    def greet(d):
        pl.semaphore_signal(barrier, inc=1, device_id=d, device_id_type=MESH)

    for d in (z_dev, xm_dev, xp_dev, core_dev, up_dev, down_dev, side_dev):
        greet(d)

    @pl.when(sp == top)
    def _():
        greet(far_up)

    @pl.when((sp == top) & (core == 1))
    def _():
        greet(dev(xx, 1 - zh, 1, up))

    @pl.when(sp == 0)
    def _():
        greet(far_down)

    @pl.when((sp == 0) & (core == 0))
    def _():
        greet(dev(xx, 1 - zh, 0, down))

    more = jnp.where(sp == top, 1 + core, 0) + jnp.where(sp == 0, 2 - core, 0)
    pl.semaphore_wait(barrier, 7 + more)

    def remote(src, dst, send, recv, d):
        return pltpu.make_async_remote_copy(
            src_ref=src, dst_ref=dst, send_sem=send, recv_sem=recv, device_id=d,
            device_id_type=MESH,
        )

    def lanes(k):
        return pl.ds(pl.multiple_of(k * L, L), L)

    def z_copy(k):
        ln = lanes(k)
        return remote(snap.at[:, :, :, ln], BZ.at[:, :, :, ln], s_z.at[k], r_z.at[k], z_dev)

    def s_copy(k):
        ln = lanes(k)
        return remote(BZ.at[:, :, :, ln], BS.at[:, :, :, ln], s_s.at[k], r_s.at[k], relay_dev)

    def xm_copy():
        return remote(snap, BP, s_x.at[0], r_x.at[0], xm_dev)

    def xp_copy():
        return remote(snap, BM, s_x.at[1], r_x.at[1], xp_dev)

    slot_of = {NATIVE: 2, XM: 0, XP: 4, ZB: 3 - 2 * zh, SB: 1 + 2 * zh}
    buffer_of = {NATIVE: snap, XM: BM, XP: BP, ZB: BZ, SB: BS}

    def span(kind, k):
        return pl.ds(0, 2048) if kind in (NATIVE, XM, XP) else lanes(k)

    def frames_of(kind, c):
        return pl.ds(4 * slot_of[kind] + 2 * c, 2)

    def local_copy(kind, k):
        ln = span(kind, k)
        return pltpu.make_async_copy(
            buffer_of[kind].at[:, pl.ds(core, 3), :, ln],
            G.at[frames_of(kind, core), pl.ds(1 - core, 3), :, ln], l_g.at[8 * kind + k],
        )

    def core_copy(kind, k):
        ln, i = span(kind, k), 8 * kind + k
        return remote(
            buffer_of[kind].at[:, pl.ds(other, 3), :, ln],
            G.at[frames_of(kind, core), pl.ds(core, 3), :, ln],
            s_g.at[i, 0], r_g.at[i, 0], core_dev,
        )

    def up_copy(kind, k):
        ln, i = span(kind, k), 8 * kind + k
        return remote(
            buffer_of[kind].at[:, 3, :, ln], G.at[frames_of(kind, core), 0, :, ln],
            s_g.at[i, 1], r_g.at[i, 1 + core], up_dev,
        )

    def down_copy(kind, k):
        ln, i = span(kind, k), 8 * kind + k
        return remote(
            buffer_of[kind].at[:, 0, :, ln], G.at[frames_of(kind, core), 3, :, ln],
            s_g.at[i, 2], r_g.at[i, 1 + core], down_dev,
        )

    def far_copies(source, kind):
        slot = 1 + 2 * zh if kind == ZB else 3 - 2 * zh
        fr = pl.ds(4 * slot + 2 * core, 2)

        @pl.when(sp == top)
        def _():
            @pl.loop(0, NP)
            def _(k):
                i = 8 * kind + k
                remote(
                    source.at[:, 3, :, lanes(k)], G.at[fr, 0, :, lanes(k)],
                    s_g.at[i, 1], r_g.at[i, 1 + core], far_up,
                ).start()

        @pl.when(sp == 0)
        def _():
            @pl.loop(0, NP)
            def _(k):
                i = 8 * kind + k
                remote(
                    source.at[:, 0, :, lanes(k)], G.at[fr, 3, :, lanes(k)],
                    s_g.at[i, 2], r_g.at[i, 1 + core], far_down,
                ).start()

    def spread(kind, k=0):
        core_copy(kind, k).start()
        if kind in (NATIVE, XM, XP):
            up_copy(kind, k).start()
            down_copy(kind, k).start()
        else:

            @pl.when(sp != top)
            def _():
                up_copy(kind, k).start()

            @pl.when(sp != 0)
            def _():
                down_copy(kind, k).start()

        local_copy(kind, k).start()

    def settle(kind, k=0):
        ln, i = span(kind, k), 8 * kind + k
        local_copy(kind, k).wait()
        theirs = G.at[frames_of(kind, other), pl.ds(1 - core, 3), :, ln]
        remote(theirs, theirs, s_g.at[i, 0], r_g.at[i, 0], core_dev).wait_recv()
        for c in range(2):
            row = G.at[frames_of(kind, c), 3 * core, :, ln]
            remote(row, row, s_g.at[i, 1], r_g.at[i, 1 + c], side_dev).wait_recv()

    def sent(kind, k=0):
        core_copy(kind, k).wait_send()
        up_copy(kind, k).wait_send()
        down_copy(kind, k).wait_send()

    def take_z(k):
        z_copy(k).wait_recv()
        s_copy(k).start()
        spread(ZB, k)

    def take_s(k):
        s_copy(k).wait_recv()
        spread(SB, k)

    def settle_far(k):
        settle(ZB, k)
        settle(SB, k)

    def out_copies(k):
        mine = pltpu.make_async_copy(
            O.at[k, pl.ds(2 * core, 2)], out.at[:, pl.ds(2 * core, 2), :, lanes(k)], l_o.at[k]
        )
        theirs = remote(
            O.at[k, pl.ds(2 * other, 2)], out.at[:, pl.ds(2 * core, 2), :, lanes(k)],
            s_o.at[k], r_o.at[k], core_dev,
        )
        return mine, theirs

    @pl.loop(0, NP)
    def _(k):
        z_copy(k).start()

    xm_copy().start()
    xp_copy().start()
    spread(NATIVE)
    far_copies(snap, ZB)
    prepare(q, flat, mixw, cb, tb, mb, wsp, band, last, mix, bias)
    xp_copy().wait_recv()
    spread(XM)
    xm_copy().wait_recv()
    spread(XP)

    @pl.when(zh == 0)
    def _():
        far_copies(BP, SB)

    @pl.when(zh == 1)
    def _():
        far_copies(BM, SB)

    for kind in (NATIVE, XM, XP):
        settle(kind)

    @pl.loop(0, NP)
    def _(i):
        features(G, H0, i, OWN, wsp, bias)

        @pl.when(i >= 3)
        def _():
            take_z(i - 3)

        @pl.when(i >= 5)
        def _():
            take_s(i - 5)

    settle_far(0)
    settle_far(1)

    @pl.loop(0, NP)
    def _(i):
        @pl.when(i + 2 < NP)
        def _():
            settle_far(i + 2)

        @pl.when(i + 5 < NP)
        def _():
            take_z(i + 5)

        @pl.when(i + 3 < NP)
        def _():
            take_s(i + 3)

        k = lax.rem(i + 1, NP)
        features(G, H0, k, FAR, wsp, bias)
        levels(H0.at[k], H1, H2, O.at[k], band, last, mix, bias)
        mine, theirs = out_copies(k)
        mine.start()
        theirs.start()

    xm_copy().wait_send()
    xp_copy().wait_send()
    for kind in (NATIVE, XM, XP):
        sent(kind)

    @pl.loop(0, NP)
    def _(k):
        z_copy(k).wait_send()
        s_copy(k).wait_send()
        sent(ZB, k)
        sent(SB, k)
        mine, theirs = out_copies(k)
        mine.wait()
        theirs.wait_send()
        into = out.at[:, pl.ds(2 * other, 2), :, lanes(k)]
        remote(into, into, s_o.at[k], r_o.at[k], core_dev).wait_recv()


def shards(snapshots, conv_weight, conv_bias, tap_weight, tap_bias, mix_weight, mix_bias):
    flat = jnp.concatenate(
        [
            jnp.pad(conv_weight.reshape(1, 32, 108), ((0, 0), (0, 0), (0, 20))),
            jnp.pad(tap_weight.reshape(3, 32, 96), ((0, 0), (0, 0), (0, 32))),
        ],
        0,
    )
    vm = pl.BlockSpec(memory_space=pltpu.VMEM)
    anywhere = pl.BlockSpec(memory_space=pl.ANY)
    dma = pltpu.SemaphoreType.DMA
    return pl.pallas_call(
        kernel,
        out_shape=jax.ShapeDtypeStruct((2, 4, 32, 2048), BF),
        in_specs=[anywhere] + [vm] * 5,
        out_specs=anywhere,
        scratch_shapes=[pltpu.VMEM((2, 4, 4, 2048), BF)] * 4
        + [
            pltpu.VMEM((20, 4, 4, 2048), BF),
            pltpu.VMEM((NP, 4, 2, 32, L), BF),
            pltpu.VMEM((64, 144), BF),
            pltpu.VMEM((5, 192, 256), BF),
            pltpu.VMEM((128, 384), BF),
            pltpu.VMEM((3, 256, 256), BF),
            pltpu.VMEM((7, 32, L), F32),
            pltpu.VMEM((NP, 2, 18, 32, L), BF),
            pltpu.VMEM((2, 8, 2, 32, L), BF),
            pltpu.VMEM((2, 6, 2, 32, L), BF),
            dma((NP,)), dma((NP,)), dma((2,)), dma((2,)), dma((NP,)), dma((NP,)),
            dma((40,)), dma((40, 3)), dma((40, 3)),
            dma((NP,)), dma((NP,)), dma((NP,)),
        ],
        compiler_params=pltpu.CompilerParams(
            collective_id=0, has_side_effects=True, vmem_limit_bytes=56 << 20
        ),
        name="encoder",
    )(snapshots, flat, mix_weight, conv_bias[None], tap_bias, mix_bias)


def solution(mesh):
    in_specs = (P("tm", "space", None, None), P(), P(), P(), P(), P(), P())
    out_specs = P("tm", "space", None, None)
    return jax.shard_map(shards, mesh=mesh, in_specs=in_specs, out_specs=out_specs, check_vma=False)
```

```python
import jax
import jax.numpy as jnp
from jax import lax
from jax.experimental import pallas as pl
from jax.experimental.pallas import tpu as pltpu
from jax.sharding import PartitionSpec as P

F32 = jnp.float32
BF = jnp.bfloat16
MESH = pl.DeviceIdType.MESH
L = 256
NP = 8
K1 = 0.7978845608028654


def iota(shape, dim):
    return lax.broadcasted_iota(jnp.int32, shape, dim)


def dot(a, b):
    return jnp.dot(a, b, preferred_element_type=F32)


def chosen(condition):
    return jnp.where(condition, 1.0, 0.0).astype(BF)


def prepare(q, flat, mixw, cb, tb, mb, wsp, band, last, mix, bias):
    j = iota((128, 144), 0)
    col = iota((128, 144), 1)
    field_row = (j * 57) >> 9
    field = (field_row * 11) >> 5
    shift = field_row - 3 * field
    match = ((j - 9 * field_row) == (col >> 4)) & (field == (col & 3)) & (j < 108)
    rows = []
    for x in range(2):
        rows.append(dot(flat[0], chosen(match & (shift == ((col >> 2) & 3) - x))))
    wsp[...] = (0.5 * jnp.concatenate(rows, 0)).astype(BF)

    def banded(weights, step, outs, ins, first, stride):
        j = iota((128, 32 * ins), 0)
        col = iota((128, 32 * ins), 1)
        gap = (iota((32 * outs, 32 * ins), 1) >> 5) - (iota((32 * outs, 32 * ins), 0) >> 5)
        total = jnp.zeros((32 * outs, 32 * ins), F32)
        for k in range(3):
            picked = dot(weights, chosen(j == 32 * k + (col & 31)))
            total = jnp.where(gap == k * step, jnp.concatenate([picked] * outs, 0), total)
        frame = first + stride * (iota((32 * outs, 32 * ins), 1) >> 5)
        return (0.5 * jnp.where((frame >= 0) & (frame < 32), total, 0.0)).astype(BF)

    for g in range(3):
        band[g] = banded(flat[1], 1, 6, 8, 4 * q - 7 + 6 * g, 1)
    for p in range(2):
        band[3 + p] = banded(flat[2], 1, 6, 8, 4 * q - 6 + p, 2)
    last[...] = banded(flat[3], 4, 4, 12, 4 * q - 4, 1)
    spread = chosen(iota((32, 256), 0) == (iota((32, 256), 1) & 31))
    same = (iota((256, 256), 0) >> 5) == (iota((256, 256), 1) >> 5)
    for s in range(3):
        tiled = jnp.concatenate([dot(mixw[s], spread)] * 8, 0)
        mix[s] = jnp.where(same, tiled, 0.0).astype(BF)
    unit = iota((32, 32), 0) == iota((32, 32), 1)
    rows = [0.5 * cb[...]] + [0.5 * tb[n : n + 1, :] for n in range(3)]
    rows += [mb[n : n + 1, :] for n in range(3)]
    for n in range(7):
        row = jnp.where(unit, jnp.broadcast_to(rows[n], (32, 32)), 0.0)
        bias[n] = jnp.broadcast_to(jnp.sum(row, 1, keepdims=True), (32, L))


def gelu(h):
    return h + h * jnp.tanh(h * (2 * K1 + (8 * K1 * 0.044715) * (h * h)))


def features(G, H0, k, frames, wsp, bias):
    left = lax.rem(2 * k + 15, 16)
    right = lax.rem(2 * k + 2, 16)
    lane = lax.rem(iota((16, 512), 1), 32)
    inner_low = chosen(lane != 0)
    inner_high = chosen(lane != 31)
    for n in frames:

        def piece(start, size):
            lanes = pl.ds(pl.multiple_of(start, 128), size)
            return jnp.concatenate([G[n + 1, r, :, lanes].astype(F32) for r in range(4)], 0)

        x = jnp.concatenate(
            [piece(left * 128, 128), piece(k * L, L), piece(right * 128, 128)], 1
        )
        x = x.astype(BF)
        planes = (pltpu.roll(x, 1, 1) * inner_low, x, pltpu.roll(x, 511, 1) * inner_high)
        moved = [(pltpu.roll(y, 32, 1), y, pltpu.roll(y, 480, 1)) for y in planes]
        taps = [moved[c][b][:, 128:384] for b in range(3) for c in range(3)]
        acc = dot(wsp[...], jnp.concatenate(taps, 0)).reshape(2, 32, L)
        h = gelu(acc + bias[0]).astype(BF)
        for x in range(2):
            H0[k, x, n] = h[x]


def levels(H0, H1, H2, O, band, last, mix, bias):
    def run(tasks, taps, finish, ahead=2):
        waiting = []
        for task in tasks:
            waiting.append((task, taps(*task)))
            if len(waiting) > ahead:
                task, acc = waiting.pop(0)
                finish(*task, acc)
        for task, acc in waiting:
            finish(*task, acc)

    def mixed(s, outs, acc):
        g = gelu(acc.reshape(outs, 32, L) + bias[1 + s]).astype(BF).reshape(outs * 32, L)
        return dot(mix[s, : outs * 32, : outs * 32], g).reshape(outs, 32, L) + bias[4 + s]

    def taps0(o0, no, x):
        xin = H0[x, o0 : o0 + no + 2].reshape((no + 2) * 32, L)
        return dot(band[o0 // 6, : no * 32, : (no + 2) * 32], xin)

    def finish0(o0, no, x, acc):
        h = (H0[x, o0 + 1 : o0 + 1 + no].astype(F32) + mixed(0, no, acc)).astype(BF)
        H1[x, o0 // 2 : (o0 + no) // 2] = h.reshape(no // 2, 2, 32, L)

    def taps1(p, x):
        return dot(band[3 + p], H1[x, :, p].reshape(256, L))

    def finish1(p, x, acc):
        H2[x, :, p] = (H1[x, 1:7, p].astype(F32) + mixed(1, 6, acc)).astype(BF)

    def taps2(x):
        return dot(last[...], H2[x].reshape(384, L))

    def finish2(x, acc):
        h = H2[x, 2:4].reshape(4, 32, L).astype(F32)
        O[:, x] = (h + mixed(2, 4, acc)).astype(BF)

    run([(o0, no, x) for o0, no in ((0, 6), (6, 6), (12, 4)) for x in range(2)], taps0, finish0)
    run([(p, x) for p in range(2) for x in range(2)], taps1, finish1)
    run([(x,) for x in range(2)], taps2, finish2)


NATIVE, XM, XP, ZB, SB = range(5)
OWN = (0, 1, 2, 7, 8, 9, 10, 15, 16, 17)
FAR = (3, 4, 5, 6, 11, 12, 13, 14)


def kernel(snap, flat, mixw, cb, tb, mb, out, BM, BP, BZ, BS, G, O, wsp, band, last, mix, bias, H0, H1, H2,
           s_z, r_z, s_x, r_x, s_s, r_s, l_g, s_g, r_g, l_o, s_o, r_o):
    tm = lax.axis_index("tm")
    sp = lax.axis_index("space")
    core = lax.rem(tm, 2)
    other = 1 - core
    zh = lax.rem(tm // 2, 2)
    xx = tm // 4
    q = 2 * xx + zh
    top = lax.axis_size("space") - 1
    up = jnp.where(sp == top, 0, sp + 1)
    down = jnp.where(sp == 0, top, sp - 1)

    def dev(x, z, c, s):
        return (lax.rem(x, 4) * 4 + z * 2 + c, s)

    z_dev = dev(xx, 1 - zh, core, sp)
    xm_dev = dev(xx + 3, zh, core, sp)
    xp_dev = dev(xx + 1, zh, core, sp)
    relay_dev = dev(xx + 1 + 2 * zh, zh, core, sp)
    core_dev = dev(xx, zh, other, sp)
    up_dev = dev(xx, zh, 0, up)
    down_dev = dev(xx, zh, 1, down)
    side_dev = dev(xx, zh, core, jnp.where(core == 0, down, up))
    far_up = dev(xx, 1 - zh, 0, up)
    far_down = dev(xx, 1 - zh, 1, down)

    barrier = pltpu.get_barrier_semaphore()

    def greet(d):
        pl.semaphore_signal(barrier, inc=1, device_id=d, device_id_type=MESH)

    for d in (z_dev, xm_dev, xp_dev, core_dev, up_dev, down_dev, side_dev):
        greet(d)

    @pl.when(sp == top)
    def _():
        greet(far_up)

    @pl.when((sp == top) & (core == 1))
    def _():
        greet(dev(xx, 1 - zh, 1, up))

    @pl.when(sp == 0)
    def _():
        greet(far_down)

    @pl.when((sp == 0) & (core == 0))
    def _():
        greet(dev(xx, 1 - zh, 0, down))

    more = jnp.where(sp == top, 1 + core, 0) + jnp.where(sp == 0, 2 - core, 0)
    pl.semaphore_wait(barrier, 7 + more)

    def remote(src, dst, send, recv, d):
        return pltpu.make_async_remote_copy(
            src_ref=src, dst_ref=dst, send_sem=send, recv_sem=recv, device_id=d,
            device_id_type=MESH,
        )

    def lanes(k):
        return pl.ds(pl.multiple_of(k * L, L), L)

    def z_copy(k):
        ln = lanes(k)
        return remote(snap.at[:, :, :, ln], BZ.at[:, :, :, ln], s_z.at[k], r_z.at[k], z_dev)

    def s_copy(k):
        ln = lanes(k)
        return remote(BZ.at[:, :, :, ln], BS.at[:, :, :, ln], s_s.at[k], r_s.at[k], relay_dev)

    def xm_copy():
        return remote(snap, BP, s_x.at[0], r_x.at[0], xm_dev)

    def xp_copy():
        return remote(snap, BM, s_x.at[1], r_x.at[1], xp_dev)

    slot_of = {NATIVE: 2, XM: 0, XP: 4, ZB: 3 - 2 * zh, SB: 1 + 2 * zh}
    buffer_of = {NATIVE: snap, XM: BM, XP: BP, ZB: BZ, SB: BS}

    def span(kind, k):
        return pl.ds(0, 2048) if kind in (NATIVE, XM, XP) else lanes(k)

    def frames_of(kind, c):
        return pl.ds(4 * slot_of[kind] + 2 * c, 2)

    def local_copy(kind, k):
        ln = span(kind, k)
        return pltpu.make_async_copy(
            buffer_of[kind].at[:, pl.ds(core, 3), :, ln],
            G.at[frames_of(kind, core), pl.ds(1 - core, 3), :, ln], l_g.at[8 * kind + k],
        )

    def core_copy(kind, k):
        ln, i = span(kind, k), 8 * kind + k
        return remote(
            buffer_of[kind].at[:, pl.ds(other, 3), :, ln],
            G.at[frames_of(kind, core), pl.ds(core, 3), :, ln],
            s_g.at[i, 0], r_g.at[i, 0], core_dev,
        )

    def up_copy(kind, k):
        ln, i = span(kind, k), 8 * kind + k
        return remote(
            buffer_of[kind].at[:, 3, :, ln], G.at[frames_of(kind, core), 0, :, ln],
            s_g.at[i, 1], r_g.at[i, 1 + core], up_dev,
        )

    def down_copy(kind, k):
        ln, i = span(kind, k), 8 * kind + k
        return remote(
            buffer_of[kind].at[:, 0, :, ln], G.at[frames_of(kind, core), 3, :, ln],
            s_g.at[i, 2], r_g.at[i, 1 + core], down_dev,
        )

    def far_copies(source, kind):
        slot = 1 + 2 * zh if kind == ZB else 3 - 2 * zh
        fr = pl.ds(4 * slot + 2 * core, 2)

        @pl.when(sp == top)
        def _():
            @pl.loop(0, NP)
            def _(k):
                i = 8 * kind + k
                remote(
                    source.at[:, 3, :, lanes(k)], G.at[fr, 0, :, lanes(k)],
                    s_g.at[i, 1], r_g.at[i, 1 + core], far_up,
                ).start()

        @pl.when(sp == 0)
        def _():
            @pl.loop(0, NP)
            def _(k):
                i = 8 * kind + k
                remote(
                    source.at[:, 0, :, lanes(k)], G.at[fr, 3, :, lanes(k)],
                    s_g.at[i, 2], r_g.at[i, 1 + core], far_down,
                ).start()

    def spread(kind, k=0):
        core_copy(kind, k).start()
        if kind in (NATIVE, XM, XP):
            up_copy(kind, k).start()
            down_copy(kind, k).start()
        else:

            @pl.when(sp != top)
            def _():
                up_copy(kind, k).start()

            @pl.when(sp != 0)
            def _():
                down_copy(kind, k).start()

        local_copy(kind, k).start()

    def settle(kind, k=0):
        ln, i = span(kind, k), 8 * kind + k
        local_copy(kind, k).wait()
        theirs = G.at[frames_of(kind, other), pl.ds(1 - core, 3), :, ln]
        remote(theirs, theirs, s_g.at[i, 0], r_g.at[i, 0], core_dev).wait_recv()
        for c in range(2):
            row = G.at[frames_of(kind, c), 3 * core, :, ln]
            remote(row, row, s_g.at[i, 1], r_g.at[i, 1 + c], side_dev).wait_recv()

    def sent(kind, k=0):
        core_copy(kind, k).wait_send()
        up_copy(kind, k).wait_send()
        down_copy(kind, k).wait_send()

    def take_z(k):
        z_copy(k).wait_recv()
        s_copy(k).start()
        spread(ZB, k)

    def take_s(k):
        s_copy(k).wait_recv()
        spread(SB, k)

    def settle_far(k):
        settle(ZB, k)
        settle(SB, k)

    def out_copies(k):
        mine = pltpu.make_async_copy(
            O.at[k, pl.ds(2 * core, 2)], out.at[:, pl.ds(2 * core, 2), :, lanes(k)], l_o.at[k]
        )
        theirs = remote(
            O.at[k, pl.ds(2 * other, 2)], out.at[:, pl.ds(2 * core, 2), :, lanes(k)],
            s_o.at[k], r_o.at[k], core_dev,
        )
        return mine, theirs

    @pl.loop(0, NP)
    def _(k):
        z_copy(k).start()

    xm_copy().start()
    xp_copy().start()
    spread(NATIVE)
    far_copies(snap, ZB)
    prepare(q, flat, mixw, cb, tb, mb, wsp, band, last, mix, bias)
    xp_copy().wait_recv()
    spread(XM)
    xm_copy().wait_recv()
    spread(XP)

    @pl.when(zh == 0)
    def _():
        far_copies(BP, SB)

    @pl.when(zh == 1)
    def _():
        far_copies(BM, SB)

    for kind in (NATIVE, XM, XP):
        settle(kind)

    @pl.loop(0, NP)
    def _(i):
        features(G, H0, i, OWN, wsp, bias)

        @pl.when(i >= 3)
        def _():
            take_z(i - 3)

        @pl.when(i >= 5)
        def _():
            take_s(i - 5)

    settle_far(0)
    settle_far(1)

    @pl.loop(0, NP)
    def _(i):
        @pl.when(i + 2 < NP)
        def _():
            settle_far(i + 2)

        @pl.when(i + 5 < NP)
        def _():
            take_z(i + 5)

        @pl.when(i + 3 < NP)
        def _():
            take_s(i + 3)

        k = lax.rem(i + 1, NP)
        features(G, H0, k, FAR, wsp, bias)
        levels(H0.at[k], H1, H2, O.at[k], band, last, mix, bias)
        mine, theirs = out_copies(k)
        mine.start()
        theirs.start()

    xm_copy().wait_send()
    xp_copy().wait_send()
    for kind in (NATIVE, XM, XP):
        sent(kind)

    @pl.loop(0, NP)
    def _(k):
        z_copy(k).wait_send()
        s_copy(k).wait_send()
        sent(ZB, k)
        sent(SB, k)
        mine, theirs = out_copies(k)
        mine.wait()
        theirs.wait_send()
        into = out.at[:, pl.ds(2 * other, 2), :, lanes(k)]
        remote(into, into, s_o.at[k], r_o.at[k], core_dev).wait_recv()


def shards(snapshots, conv_weight, conv_bias, tap_weight, tap_bias, mix_weight, mix_bias):
    flat = jnp.concatenate(
        [
            jnp.pad(conv_weight.reshape(1, 32, 108), ((0, 0), (0, 0), (0, 20))),
            jnp.pad(tap_weight.reshape(3, 32, 96), ((0, 0), (0, 0), (0, 32))),
        ],
        0,
    )
    vm = pl.BlockSpec(memory_space=pltpu.VMEM)
    anywhere = pl.BlockSpec(memory_space=pl.ANY)
    dma = pltpu.SemaphoreType.DMA
    return pl.pallas_call(
        kernel,
        out_shape=pltpu.VMEM((2, 4, 32, 2048), BF),
        in_specs=[anywhere] + [vm] * 5,
        out_specs=vm,
        scratch_shapes=[pltpu.VMEM((2, 4, 4, 2048), BF)] * 4
        + [
            pltpu.VMEM((20, 4, 4, 2048), BF),
            pltpu.VMEM((NP, 4, 2, 32, L), BF),
            pltpu.VMEM((64, 144), BF),
            pltpu.VMEM((5, 192, 256), BF),
            pltpu.VMEM((128, 384), BF),
            pltpu.VMEM((3, 256, 256), BF),
            pltpu.VMEM((7, 32, L), F32),
            pltpu.VMEM((NP, 2, 18, 32, L), BF),
            pltpu.VMEM((2, 8, 2, 32, L), BF),
            pltpu.VMEM((2, 6, 2, 32, L), BF),
            dma((NP,)), dma((NP,)), dma((2,)), dma((2,)), dma((NP,)), dma((NP,)),
            dma((40,)), dma((40, 3)), dma((40, 3)),
            dma((NP,)), dma((NP,)), dma((NP,)),
        ],
        compiler_params=pltpu.CompilerParams(
            collective_id=0, has_side_effects=True, vmem_limit_bytes=56 << 20
        ),
        name="encoder",
    )(snapshots, flat, mix_weight, conv_bias[None], tap_bias, mix_bias)


def solution(mesh):
    in_specs = (P("tm", "space", None, None), P(), P(), P(), P(), P(), P())
    out_specs = P("tm", "space", None, None)
    return jax.shard_map(shards, mesh=mesh, in_specs=in_specs, out_specs=out_specs, check_vma=False)
```

```python
import jax
import jax.numpy as jnp
from jax import lax
from jax.experimental import pallas as pl
from jax.experimental.pallas import tpu as pltpu
from jax.sharding import PartitionSpec as P

F32 = jnp.float32
BF = jnp.bfloat16
MESH = pl.DeviceIdType.MESH
L = 256
NP = 8
K1 = 0.7978845608028654


def iota(shape, dim):
    return lax.broadcasted_iota(jnp.int32, shape, dim)


def dot(a, b):
    return jnp.dot(a, b, preferred_element_type=F32)


def chosen(condition):
    return jnp.where(condition, 1.0, 0.0).astype(BF)


def prepare(q, flat, mixw, cb, tb, mb, wsp, band, last, mix, bias):
    j = iota((128, 144), 0)
    col = iota((128, 144), 1)
    field_row = (j * 57) >> 9
    field = (field_row * 11) >> 5
    shift = field_row - 3 * field
    match = ((j - 9 * field_row) == (col >> 4)) & (field == (col & 3)) & (j < 108)
    rows = []
    for x in range(2):
        rows.append(dot(flat[0], chosen(match & (shift == ((col >> 2) & 3) - x))))
    wsp[...] = (0.5 * jnp.concatenate(rows, 0)).astype(BF)

    def banded(weights, step, outs, ins, first, stride):
        j = iota((128, 32 * ins), 0)
        col = iota((128, 32 * ins), 1)
        gap = (iota((32 * outs, 32 * ins), 1) >> 5) - (iota((32 * outs, 32 * ins), 0) >> 5)
        total = jnp.zeros((32 * outs, 32 * ins), F32)
        for k in range(3):
            picked = dot(weights, chosen(j == 32 * k + (col & 31)))
            total = jnp.where(gap == k * step, jnp.concatenate([picked] * outs, 0), total)
        frame = first + stride * (iota((32 * outs, 32 * ins), 1) >> 5)
        return (0.5 * jnp.where((frame >= 0) & (frame < 32), total, 0.0)).astype(BF)

    for g in range(3):
        band[g] = banded(flat[1], 1, 6, 8, 4 * q - 7 + 6 * g, 1)
    for p in range(2):
        band[3 + p] = banded(flat[2], 1, 6, 8, 4 * q - 6 + p, 2)
    last[...] = banded(flat[3], 4, 4, 12, 4 * q - 4, 1)
    spread = chosen(iota((32, 256), 0) == (iota((32, 256), 1) & 31))
    same = (iota((256, 256), 0) >> 5) == (iota((256, 256), 1) >> 5)
    for s in range(3):
        tiled = jnp.concatenate([dot(mixw[s], spread)] * 8, 0)
        mix[s] = jnp.where(same, tiled, 0.0).astype(BF)
    unit = iota((32, 32), 0) == iota((32, 32), 1)
    rows = [0.5 * cb[...]] + [0.5 * tb[n : n + 1, :] for n in range(3)]
    rows += [mb[n : n + 1, :] for n in range(3)]
    for n in range(7):
        row = jnp.where(unit, jnp.broadcast_to(rows[n], (32, 32)), 0.0)
        bias[n] = jnp.broadcast_to(jnp.sum(row, 1, keepdims=True), (32, L))


def gelu(h):
    return h + h * jnp.tanh(h * (2 * K1 + (8 * K1 * 0.044715) * (h * h)))


def features(G, H0, k, frames, wsp, bias):
    left = lax.rem(2 * k + 15, 16)
    right = lax.rem(2 * k + 2, 16)
    lane = lax.rem(iota((16, 512), 1), 32)
    inner_low = chosen(lane != 0)
    inner_high = chosen(lane != 31)
    for n in frames:

        def piece(start, size):
            lanes = pl.ds(pl.multiple_of(start, 128), size)
            return jnp.concatenate([G[n + 1, r, :, lanes].astype(F32) for r in range(4)], 0)

        x = jnp.concatenate(
            [piece(left * 128, 128), piece(k * L, L), piece(right * 128, 128)], 1
        )
        x = x.astype(BF)
        planes = (pltpu.roll(x, 1, 1) * inner_low, x, pltpu.roll(x, 511, 1) * inner_high)
        moved = [(pltpu.roll(y, 32, 1), y, pltpu.roll(y, 480, 1)) for y in planes]
        taps = [moved[c][b][:, 128:384] for b in range(3) for c in range(3)]
        acc = dot(wsp[...], jnp.concatenate(taps, 0)).reshape(2, 32, L)
        h = gelu(acc + bias[0]).astype(BF)
        for x in range(2):
            H0[k, x, n] = h[x]


def levels(H0, H1, H2, O, band, last, mix, bias):
    def run(tasks, taps, finish, ahead=2):
        waiting = []
        for task in tasks:
            waiting.append((task, taps(*task)))
            if len(waiting) > ahead:
                task, acc = waiting.pop(0)
                finish(*task, acc)
        for task, acc in waiting:
            finish(*task, acc)

    def mixed(s, outs, acc):
        g = gelu(acc.reshape(outs, 32, L) + bias[1 + s]).astype(BF).reshape(outs * 32, L)
        return dot(mix[s, : outs * 32, : outs * 32], g).reshape(outs, 32, L) + bias[4 + s]

    def taps0(o0, no, x):
        xin = H0[x, o0 : o0 + no + 2].reshape((no + 2) * 32, L)
        return dot(band[o0 // 6, : no * 32, : (no + 2) * 32], xin)

    def finish0(o0, no, x, acc):
        h = (H0[x, o0 + 1 : o0 + 1 + no].astype(F32) + mixed(0, no, acc)).astype(BF)
        H1[x, o0 // 2 : (o0 + no) // 2] = h.reshape(no // 2, 2, 32, L)

    def taps1(p, x):
        return dot(band[3 + p], H1[x, :, p].reshape(256, L))

    def finish1(p, x, acc):
        H2[x, :, p] = (H1[x, 1:7, p].astype(F32) + mixed(1, 6, acc)).astype(BF)

    def taps2(x):
        return dot(last[...], H2[x].reshape(384, L))

    def finish2(x, acc):
        h = H2[x, 2:4].reshape(4, 32, L).astype(F32)
        O[:, x] = (h + mixed(2, 4, acc)).astype(BF)

    run([(o0, no, x) for o0, no in ((0, 6), (6, 6), (12, 4)) for x in range(2)], taps0, finish0)
    run([(p, x) for p in range(2) for x in range(2)], taps1, finish1)
    run([(x,) for x in range(2)], taps2, finish2)


NATIVE, XM, XP, ZB, SB = range(5)
OWN = (0, 1, 2, 7, 8, 9, 10, 15, 16, 17)
FAR = (3, 4, 5, 6, 11, 12, 13, 14)


def kernel(snap, flat, mixw, cb, tb, mb, out, BM, BP, BZ, BS, G, O, wsp, band, last, mix, bias, H0, H1, H2,
           s_z, r_z, s_x, r_x, s_s, r_s, l_g, s_g, r_g, l_o, s_o, r_o):
    tm = lax.axis_index("tm")
    sp = lax.axis_index("space")
    core = lax.rem(tm, 2)
    other = 1 - core
    zh = lax.rem(tm // 2, 2)
    xx = tm // 4
    q = 2 * xx + zh
    top = lax.axis_size("space") - 1
    up = jnp.where(sp == top, 0, sp + 1)
    down = jnp.where(sp == 0, top, sp - 1)

    def dev(x, z, c, s):
        return (lax.rem(x, 4) * 4 + z * 2 + c, s)

    z_dev = dev(xx, 1 - zh, core, sp)
    xm_dev = dev(xx + 3, zh, core, sp)
    xp_dev = dev(xx + 1, zh, core, sp)
    relay_dev = dev(xx + 1 + 2 * zh, zh, core, sp)
    core_dev = dev(xx, zh, other, sp)
    up_dev = dev(xx, zh, 0, up)
    down_dev = dev(xx, zh, 1, down)
    side_dev = dev(xx, zh, core, jnp.where(core == 0, down, up))
    far_up = dev(xx, 1 - zh, 0, up)
    far_down = dev(xx, 1 - zh, 1, down)

    barrier = pltpu.get_barrier_semaphore()

    def greet(d):
        pl.semaphore_signal(barrier, inc=1, device_id=d, device_id_type=MESH)

    for d in (z_dev, xm_dev, xp_dev, core_dev, up_dev, down_dev, side_dev):
        greet(d)

    @pl.when(sp == top)
    def _():
        greet(far_up)

    @pl.when((sp == top) & (core == 1))
    def _():
        greet(dev(xx, 1 - zh, 1, up))

    @pl.when(sp == 0)
    def _():
        greet(far_down)

    @pl.when((sp == 0) & (core == 0))
    def _():
        greet(dev(xx, 1 - zh, 0, down))

    more = jnp.where(sp == top, 1 + core, 0) + jnp.where(sp == 0, 2 - core, 0)
    pl.semaphore_wait(barrier, 7 + more)

    def remote(src, dst, send, recv, d):
        return pltpu.make_async_remote_copy(
            src_ref=src, dst_ref=dst, send_sem=send, recv_sem=recv, device_id=d,
            device_id_type=MESH,
        )

    def lanes(k):
        return pl.ds(pl.multiple_of(k * L, L), L)

    def z_copy(k):
        ln = lanes(k)
        return remote(snap.at[:, :, :, ln], BZ.at[:, :, :, ln], s_z.at[k], r_z.at[k], z_dev)

    def s_copy(k):
        ln = lanes(k)
        return remote(BZ.at[:, :, :, ln], BS.at[:, :, :, ln], s_s.at[k], r_s.at[k], relay_dev)

    def xm_copy():
        return remote(snap, BP, s_x.at[0], r_x.at[0], xm_dev)

    def xp_copy():
        return remote(snap, BM, s_x.at[1], r_x.at[1], xp_dev)

    slot_of = {NATIVE: 2, XM: 0, XP: 4, ZB: 3 - 2 * zh, SB: 1 + 2 * zh}
    buffer_of = {NATIVE: snap, XM: BM, XP: BP, ZB: BZ, SB: BS}

    def span(kind, k):
        return pl.ds(0, 2048) if kind in (NATIVE, XM, XP) else lanes(k)

    def frames_of(kind, c):
        return pl.ds(4 * slot_of[kind] + 2 * c, 2)

    def local_copy(kind, k):
        ln = span(kind, k)
        return pltpu.make_async_copy(
            buffer_of[kind].at[:, pl.ds(core, 3), :, ln],
            G.at[frames_of(kind, core), pl.ds(1 - core, 3), :, ln], l_g.at[8 * kind + k],
        )

    def core_copy(kind, k):
        ln, i = span(kind, k), 8 * kind + k
        return remote(
            buffer_of[kind].at[:, pl.ds(other, 3), :, ln],
            G.at[frames_of(kind, core), pl.ds(core, 3), :, ln],
            s_g.at[i, 0], r_g.at[i, 0], core_dev,
        )

    def up_copy(kind, k):
        ln, i = span(kind, k), 8 * kind + k
        return remote(
            buffer_of[kind].at[:, 3, :, ln], G.at[frames_of(kind, core), 0, :, ln],
            s_g.at[i, 1], r_g.at[i, 1 + core], up_dev,
        )

    def down_copy(kind, k):
        ln, i = span(kind, k), 8 * kind + k
        return remote(
            buffer_of[kind].at[:, 0, :, ln], G.at[frames_of(kind, core), 3, :, ln],
            s_g.at[i, 2], r_g.at[i, 1 + core], down_dev,
        )

    def far_copies(source, kind):
        slot = 1 + 2 * zh if kind == ZB else 3 - 2 * zh
        fr = pl.ds(4 * slot + 2 * core, 2)

        @pl.when(sp == top)
        def _():
            @pl.loop(0, NP)
            def _(k):
                i = 8 * kind + k
                remote(
                    source.at[:, 3, :, lanes(k)], G.at[fr, 0, :, lanes(k)],
                    s_g.at[i, 1], r_g.at[i, 1 + core], far_up,
                ).start()

        @pl.when(sp == 0)
        def _():
            @pl.loop(0, NP)
            def _(k):
                i = 8 * kind + k
                remote(
                    source.at[:, 0, :, lanes(k)], G.at[fr, 3, :, lanes(k)],
                    s_g.at[i, 2], r_g.at[i, 1 + core], far_down,
                ).start()

    def spread(kind, k=0):
        core_copy(kind, k).start()
        if kind in (NATIVE, XM, XP):
            up_copy(kind, k).start()
            down_copy(kind, k).start()
        else:

            @pl.when(sp != top)
            def _():
                up_copy(kind, k).start()

            @pl.when(sp != 0)
            def _():
                down_copy(kind, k).start()

        local_copy(kind, k).start()

    def settle(kind, k=0):
        ln, i = span(kind, k), 8 * kind + k
        local_copy(kind, k).wait()
        theirs = G.at[frames_of(kind, other), pl.ds(1 - core, 3), :, ln]
        remote(theirs, theirs, s_g.at[i, 0], r_g.at[i, 0], core_dev).wait_recv()
        for c in range(2):
            row = G.at[frames_of(kind, c), 3 * core, :, ln]
            remote(row, row, s_g.at[i, 1], r_g.at[i, 1 + c], side_dev).wait_recv()

    def sent(kind, k=0):
        core_copy(kind, k).wait_send()
        up_copy(kind, k).wait_send()
        down_copy(kind, k).wait_send()

    def take_z(k):
        z_copy(k).wait_recv()
        s_copy(k).start()
        spread(ZB, k)

    def take_s(k):
        s_copy(k).wait_recv()
        spread(SB, k)

    def settle_far(k):
        settle(ZB, k)
        settle(SB, k)

    def out_copies(k):
        mine = pltpu.make_async_copy(
            O.at[k, pl.ds(2 * core, 2)], out.at[:, pl.ds(2 * core, 2), :, lanes(k)], l_o.at[k]
        )
        theirs = remote(
            O.at[k, pl.ds(2 * other, 2)], out.at[:, pl.ds(2 * core, 2), :, lanes(k)],
            s_o.at[k], r_o.at[k], core_dev,
        )
        return mine, theirs

    @pl.loop(0, NP)
    def _(k):
        z_copy(k).start()

    xm_copy().start()
    xp_copy().start()
    spread(NATIVE)
    far_copies(snap, ZB)
    prepare(q, flat, mixw, cb, tb, mb, wsp, band, last, mix, bias)
    xp_copy().wait_recv()
    spread(XM)
    xm_copy().wait_recv()
    spread(XP)

    @pl.when(zh == 0)
    def _():
        far_copies(BP, SB)

    @pl.when(zh == 1)
    def _():
        far_copies(BM, SB)

    for kind in (NATIVE, XM, XP):
        settle(kind)

    @pl.loop(0, NP)
    def _(i):
        features(G, H0, i, OWN, wsp, bias)

    @pl.loop(0, 5)
    def _(i):
        take_z(i)

        @pl.when(i >= 2)
        def _():
            take_s(i - 2)

    settle_far(0)
    settle_far(1)

    @pl.loop(0, NP)
    def _(i):
        @pl.when(i + 5 < NP)
        def _():
            take_z(i + 5)

        @pl.when(i + 3 < NP)
        def _():
            take_s(i + 3)

        @pl.when(i + 2 < NP)
        def _():
            settle_far(i + 2)

        k = lax.rem(i + 1, NP)
        features(G, H0, k, FAR, wsp, bias)
        levels(H0.at[k], H1, H2, O.at[k], band, last, mix, bias)
        mine, theirs = out_copies(k)
        mine.start()
        theirs.start()

    xm_copy().wait_send()
    xp_copy().wait_send()
    for kind in (NATIVE, XM, XP):
        sent(kind)

    @pl.loop(0, NP)
    def _(k):
        z_copy(k).wait_send()
        s_copy(k).wait_send()
        sent(ZB, k)
        sent(SB, k)
        mine, theirs = out_copies(k)
        mine.wait()
        theirs.wait_send()
        into = out.at[:, pl.ds(2 * other, 2), :, lanes(k)]
        remote(into, into, s_o.at[k], r_o.at[k], core_dev).wait_recv()


def shards(snapshots, conv_weight, conv_bias, tap_weight, tap_bias, mix_weight, mix_bias):
    flat = jnp.concatenate(
        [
            jnp.pad(conv_weight.reshape(1, 32, 108), ((0, 0), (0, 0), (0, 20))),
            jnp.pad(tap_weight.reshape(3, 32, 96), ((0, 0), (0, 0), (0, 32))),
        ],
        0,
    )
    vm = pl.BlockSpec(memory_space=pltpu.VMEM)
    anywhere = pl.BlockSpec(memory_space=pl.ANY)
    dma = pltpu.SemaphoreType.DMA
    return pl.pallas_call(
        kernel,
        out_shape=pltpu.VMEM((2, 4, 32, 2048), BF),
        in_specs=[anywhere] + [vm] * 5,
        out_specs=vm,
        scratch_shapes=[pltpu.VMEM((2, 4, 4, 2048), BF)] * 4
        + [
            pltpu.VMEM((20, 4, 4, 2048), BF),
            pltpu.VMEM((NP, 4, 2, 32, L), BF),
            pltpu.VMEM((64, 144), BF),
            pltpu.VMEM((5, 192, 256), BF),
            pltpu.VMEM((128, 384), BF),
            pltpu.VMEM((3, 256, 256), BF),
            pltpu.VMEM((7, 32, L), F32),
            pltpu.VMEM((NP, 2, 18, 32, L), BF),
            pltpu.VMEM((2, 8, 2, 32, L), BF),
            pltpu.VMEM((2, 6, 2, 32, L), BF),
            dma((NP,)), dma((NP,)), dma((2,)), dma((2,)), dma((NP,)), dma((NP,)),
            dma((40,)), dma((40, 3)), dma((40, 3)),
            dma((NP,)), dma((NP,)), dma((NP,)),
        ],
        compiler_params=pltpu.CompilerParams(
            collective_id=0, has_side_effects=True, vmem_limit_bytes=56 << 20
        ),
        name="encoder",
    )(snapshots, flat, mix_weight, conv_bias[None], tap_bias, mix_bias)


def solution(mesh):
    in_specs = (P("tm", "space", None, None), P(), P(), P(), P(), P(), P())
    out_specs = P("tm", "space", None, None)
    return jax.shard_map(shards, mesh=mesh, in_specs=in_specs, out_specs=out_specs, check_vma=False)
```
